32 devices in a mesh: dp: 4 (over z), seq: 8 (over y, x, core).
Axes of the slice: x: 2, y: 2, z: 4, core: 2. Of those that a mesh axis runs over, the one named last changes fastest.
Arguments:
- inputs: bfloat16 [4, 65536, 512], P('dp', 'seq'), may hold values from -6 to 6
- cotangent: bfloat16 [4, 65536, 512], P('dp', 'seq'), may hold values from -6 to 6
- value_weight: bfloat16 [512, 512], replicated, may hold values from -0.25 to 0.25
- gate_weight: bfloat16 [512, 512], replicated, may hold values from -0.25 to 0.25
- first_blocks: bfloat16 [256, 256, 256], P('seq'), may hold values from -0.375 to 0.375
- second_blocks: bfloat16 [256, 256, 256], P('seq'), may hold values from -0.375 to 0.375
Outputs:
- grad_inputs: bfloat16 [4, 65536, 512], P('dp', 'seq')
- grad_value_weight: float32 [512, 512], replicated
- grad_gate_weight: float32 [512, 512], replicated
- grad_first_blocks: float32 [256, 256, 256], P('seq')
- grad_second_blocks: float32 [256, 256, 256], P('seq')
The draws below stay inside these ranges and needn't reach their ends.
All inputs are finite; a program needn't handle non-finite values.
Results may differ from the reference program's by a relative error of at most 0.014.
Values may be sent and summed in bfloat16 or wider, within the bound.
A program may use at most 256 MiB of HBM per device.

```python
import jax
import jax.numpy as jnp
from jax import lax

D = 512
BLOCK_P = 256
BLOCK_A = 256
SEQS = 4
LENGTH = 65536


def steps_of(rng, dims, split, low, top_value):
    factor_of = 1.0
    for axis_at, shards_of in split:
        draws = jax.random.uniform(jax.random.fold_in(jax.random.fold_in(rng, 6), axis_at), (shards_of,), jnp.float32, low / len(split), top_value / len(split))
        factor_of = factor_of * jnp.repeat(jnp.exp(draws), dims[axis_at] // shards_of).reshape((-1,) + (1,) * (len(dims) - 1 - axis_at))
    return factor_of


def noise(stream_key, extent, scale, bound, pieces=(), dtype=jnp.bfloat16):
    entries = scale * jax.random.normal(stream_key, extent, jnp.float32)
    if pieces:
        entries = entries * steps_of(stream_key, extent, pieces, -0.22, 0.18)
    return jnp.clip(entries, -bound, bound).astype(dtype)


def setup_inputs(seed: int = 0) -> dict:
    arg_keys = jax.random.split(jax.random.key(seed), 7)
    inputs = noise(arg_keys[0], (SEQS, LENGTH, D), 1.0, 6.0, ((0, 4), (1, 8)))
    cotangent = noise(arg_keys[1], (SEQS, LENGTH, D), 1.0, 6.0, ((0, 4), (1, 8)))
    value_weight = noise(arg_keys[2], (D, D), D ** -0.5, 0.25)
    gate_weight = noise(arg_keys[3], (D, D), D ** -0.5, 0.25)
    first_blocks = noise(arg_keys[4], (BLOCK_A, BLOCK_P, BLOCK_P), BLOCK_P ** -0.5, 0.375, ((0, 8),))
    second_blocks = noise(arg_keys[5], (BLOCK_P, BLOCK_A, BLOCK_A), BLOCK_A ** -0.5, 0.375, ((0, 8),))
    return {"inputs": inputs, "cotangent": cotangent, "value_weight": value_weight, "gate_weight": gate_weight, "first_blocks": first_blocks, "second_blocks": second_blocks}


def one_sequence(carry, pair):
    seq_in, seq_cot = pair
    value_weight, gate_weight, first_blocks, second_blocks = carry[4:]
    values = jnp.dot(seq_in, value_weight, preferred_element_type=jnp.float32).astype(jnp.bfloat16)
    gate_rows = jnp.dot(seq_in, gate_weight, preferred_element_type=jnp.float32).astype(jnp.bfloat16)
    value_blk = values.reshape(BLOCK_A, BLOCK_P, D)
    first_mix = jnp.einsum('aqp,apd->aqd', first_blocks.astype(jnp.float32), value_blk.astype(jnp.float32)).astype(jnp.bfloat16)
    second_mix = jnp.einsum('pba,apd->bpd', second_blocks.astype(jnp.float32), first_mix.astype(jnp.float32)).astype(jnp.bfloat16)
    cot_f = seq_cot.astype(jnp.float32)
    grad_mix = (cot_f * gate_rows.astype(jnp.float32)).astype(jnp.bfloat16).reshape(BLOCK_A, BLOCK_P, D)
    grad_gates = (cot_f * second_mix.reshape(LENGTH, D).astype(jnp.float32)).astype(jnp.bfloat16)
    grad_first_mix = jnp.einsum('pba,bpd->apd', second_blocks.astype(jnp.float32), grad_mix.astype(jnp.float32)).astype(jnp.bfloat16)
    grad_second = jnp.einsum('bpd,apd->pba', grad_mix.astype(jnp.float32), first_mix.astype(jnp.float32))
    grad_values = jnp.einsum('aqp,aqd->apd', first_blocks.astype(jnp.float32), grad_first_mix.astype(jnp.float32)).astype(jnp.bfloat16)
    grad_first = jnp.einsum('aqd,apd->aqp', grad_first_mix.astype(jnp.float32), value_blk.astype(jnp.float32))
    flat_gv = grad_values.reshape(LENGTH, D)
    contract = (((0,), (0,)), ((), ()))
    w_val = lax.dot_general(seq_in, flat_gv, contract, preferred_element_type=jnp.float32)
    w_gate = lax.dot_general(seq_in, grad_gates, contract, preferred_element_type=jnp.float32)
    back = (((1,), (1,)), ((), ()))
    grad_in = (lax.dot_general(flat_gv, value_weight, back, preferred_element_type=jnp.float32) + lax.dot_general(grad_gates, gate_weight, back, preferred_element_type=jnp.float32)).astype(jnp.bfloat16)
    new_carry = (carry[0] + w_val, carry[1] + w_gate, carry[2] + grad_first, carry[3] + grad_second) + carry[4:]
    return (new_carry, grad_in)

def reference(inputs, cotangent, value_weight, gate_weight, first_blocks, second_blocks):
    start = (jnp.zeros((D, D), jnp.float32), jnp.zeros((D, D), jnp.float32), jnp.zeros((BLOCK_A, BLOCK_P, BLOCK_P), jnp.float32), jnp.zeros((BLOCK_P, BLOCK_A, BLOCK_A), jnp.float32), value_weight, gate_weight, first_blocks, second_blocks)
    final, grad_inputs = lax.scan(one_sequence, start, (inputs, cotangent))
    weight_scale = 1.0 / jnp.sqrt(jnp.float32(SEQS * LENGTH))
    block_scale = 1.0 / jnp.sqrt(jnp.float32(SEQS * D))
    return (grad_inputs, final[0] * weight_scale, final[1] * weight_scale, final[2] * block_scale, final[3] * block_scale)
```

```python
import jax
import jax.numpy as jnp
from jax import lax
from jax.experimental import pallas as pl
from jax.sharding import PartitionSpec as P

BF = jnp.bfloat16
F32 = jnp.float32


def packed_grad_mix(x, cot, weight, blocks, n):
    rows, channels = x.shape
    length = rows // blocks
    own = length // n

    def body(x_ref, c_ref, w_ref, o_ref):
        gate = jnp.dot(x_ref[...], w_ref[...], preferred_element_type=F32).astype(BF)
        mix = (c_ref[...].astype(F32) * gate.astype(F32)).astype(BF)
        o_ref[...] = mix.reshape(n, 1, own, channels)

    return pl.pallas_call(
        body,
        out_shape=jax.ShapeDtypeStruct((n, blocks, own, channels), BF),
        grid=(blocks,),
        in_specs=[
            pl.BlockSpec((length, channels), lambda a: (a, 0)),
            pl.BlockSpec((length, channels), lambda a: (a, 0)),
            pl.BlockSpec((channels, channels), lambda a: (0, 0)),
        ],
        out_specs=pl.BlockSpec((n, 1, own, channels), lambda a: (0, a, 0, 0)),
        cost_estimate=pl.CostEstimate(
            flops=2 * rows * channels * channels, bytes_accessed=6 * rows * channels, transcendentals=0
        ),
    )(x, cot, weight)


def packed_first_mix(factor, values, order, n):
    blocks, length, channels = values.shape
    own = length // n

    def body(f_ref, v_ref, _, o_ref):
        mix = jnp.dot(f_ref[0], v_ref[0], preferred_element_type=F32).astype(BF)
        o_ref[...] = mix.reshape(n, 1, own, channels)

    return pl.pallas_call(
        body,
        out_shape=jax.ShapeDtypeStruct((n, blocks, own, channels), BF),
        grid=(blocks,),
        in_specs=[
            pl.BlockSpec((1, length, length), lambda a: (a, 0, 0)),
            pl.BlockSpec((1, length, channels), lambda a: (a, 0, 0)),
            pl.BlockSpec(memory_space=pl.ANY),
        ],
        out_specs=pl.BlockSpec((n, 1, own, channels), lambda a: (0, a, 0, 0)),
        cost_estimate=pl.CostEstimate(
            flops=2 * blocks * length * length * channels,
            bytes_accessed=5 * blocks * length * channels,
            transcendentals=0,
        ),
    )(factor, values, order)


def nought(x):
    return jnp.minimum(jnp.abs(x[(0,) * x.ndim]), 0).astype(x.dtype)


def dp_sum(x):
    n = lax.axis_size("dp")
    me = lax.axis_index("dp")
    parts = x.reshape((n, x.shape[0] // n) + x.shape[1:])

    def shift(v, by):
        return lax.ppermute(v, "dp", [(i, (i + by) % n) for i in range(n)])

    total = lax.dynamic_index_in_dim(parts, me, 0, keepdims=False).astype(F32)
    got = [
        shift(lax.dynamic_index_in_dim(parts, (me + by) % n, 0, keepdims=False), by)
        for by in range(1, n)
    ]
    for g in got:
        total = total + g.astype(F32)
    total = total.astype(BF)
    out = jnp.zeros(parts.shape, F32)
    out = lax.dynamic_update_index_in_dim(out, total.astype(F32), me, 0)
    for by in range(1, n):
        out = lax.dynamic_update_index_in_dim(
            out, shift(total, by).astype(F32), (me - by + n) % n, 0
        )
    return out.reshape(x.shape), total


def whole_sum(x):
    n = lax.axis_size("seq")
    rows = lax.all_to_all(
        x.reshape((n, x.shape[0] // n) + x.shape[1:]), "seq", split_axis=0, concat_axis=0, tiled=True
    )
    mine = jnp.sum(rows, axis=0)
    mine = jnp.sum(lax.all_gather(mine, "dp"), axis=0)
    return lax.all_gather(mine, "seq", tiled=True)


def on_device(inputs, cotangent, value_weight, gate_weight, first_blocks, second_blocks):
    groups, own_tokens, channels = inputs.shape
    own_blocks, block_len, _ = first_blocks.shape
    n_seq = lax.axis_size("seq")
    own_p = block_len // n_seq
    rows = groups * own_tokens
    flat_in = inputs.reshape(rows, channels)
    cot_flat = cotangent.reshape(rows, channels)

    def exchange(x):
        return lax.all_to_all(x, "seq", split_axis=0, concat_axis=0, tiled=True)

    def to_p(x):
        return exchange(x).reshape(-1, own_p, channels)

    def to_a(x):
        got = exchange(x.reshape(n_seq, own_blocks, own_p, channels))
        return got.transpose(1, 0, 2, 3).reshape(own_blocks, block_len, channels)

    grad_mix = packed_grad_mix(flat_in, cot_flat, gate_weight, own_blocks, n_seq)
    spread_grad = to_p(grad_mix)

    values = jnp.dot(flat_in, value_weight, preferred_element_type=F32).astype(BF)
    value_blk = values.reshape(own_blocks, block_len, channels)
    spread_mix = to_p(packed_first_mix(first_blocks, value_blk, spread_grad, n_seq))

    gfm = jnp.einsum("pba,bpd->apd", second_blocks, spread_grad, preferred_element_type=F32)
    grad_first_mix = to_a(gfm.astype(BF))

    total_rows = rows * lax.axis_size("dp") * n_seq
    weight_scale = 1.0 / jnp.sqrt(F32(total_rows))
    block_scale = 1.0 / jnp.sqrt(F32(lax.axis_size("dp") * channels))

    grad_second = jnp.einsum("bpd,apd->pba", spread_grad, spread_mix, preferred_element_type=F32)
    grad_second = (grad_second * block_scale).astype(BF)
    smix = jnp.einsum("pba,apd->bpd", second_blocks + nought(grad_second), spread_mix, preferred_element_type=F32)
    second_mix = to_a(smix.astype(BF))
    grad_second = lax.psum(grad_second, "dp")

    grad_first = jnp.einsum("aqd,apd->aqp", grad_first_mix, value_blk, preferred_element_type=F32)
    grad_first = (grad_first * block_scale).astype(BF)
    grad_first, share = dp_sum(grad_first)
    later = nought(share).astype(F32)

    grad_values = jnp.einsum(
        "aqp,aqd->apd", first_blocks, grad_first_mix, preferred_element_type=F32
    ).astype(BF)
    flat_gv = grad_values.reshape(rows, channels)
    contract = (((0,), (0,)), ((), ()))
    backward = (((1,), (1,)), ((), ()))
    w_val = lax.dot_general(flat_in, flat_gv, contract, preferred_element_type=F32)

    grad_gates = (cot_flat.astype(F32) * (second_mix.reshape(rows, channels).astype(F32) + later)).astype(BF)
    w_gate = lax.dot_general(flat_in, grad_gates, contract, preferred_element_type=F32)
    w_val, w_gate = jnp.split(whole_sum(jnp.concatenate([w_val, w_gate]) * weight_scale), 2)
    grad_in = (
        lax.dot_general(flat_gv, value_weight, backward, preferred_element_type=F32)
        + lax.dot_general(grad_gates, gate_weight, backward, preferred_element_type=F32)
    ).astype(BF)
    return (
        grad_in.reshape(inputs.shape),
        w_val,
        w_gate,
        grad_first,
        grad_second.astype(F32),
    )


def solution(mesh):
    placed = (
        P("dp", "seq", None),
        P("dp", "seq", None),
        P(),
        P(),
        P("seq", None, None),
        P("seq", None, None),
    )
    return jax.shard_map(
        on_device,
        mesh=mesh,
        in_specs=placed,
        out_specs=(P("dp", "seq", None), P(), P(), P("seq", None, None), P("seq", None, None)),
        check_vma=False,
    )
```
